256 devices in a mesh: row: 32 (over x, z), feat: 8 (over y, core).
Axes of the slice: x: 4, y: 4, z: 8, core: 2. Of those that a mesh axis runs over, the one named last changes fastest.
Arguments:
- predictor: float32 [131072], P(('row', 'feat')), may hold values from -3 to 3
- events: int32 [131072], P(('row', 'feat')), may hold values 0 or 1
- tie_groups: int32 [131072], P(('row', 'feat')), may hold values from 7 to 131071, as said below
- node_ids: int32 [131072], P('row'), may hold values from 0 to 7
- bin_index: int32 [512, 131072], P('feat', 'row'), may hold values from 0 to 255
Outputs:
- gradient: float32 [131072], P(('row', 'feat'))
- hessian: float32 [131072], P(('row', 'feat'))
- split_gain: float32 [8, 512, 256], P(None, 'feat', 'row')
The draws below stay inside these ranges and needn't reach their ends.
Inputs may be any that keep to these rules, and one draw needn't show every extreme that they name: tie_groups never falls along the rows; each value names a run of 1 to 8 consecutive rows, some run has exactly 8, and a new run begins at every multiple of 8 rows.
All inputs are finite; a program needn't handle non-finite values. No bound on the sum of `events` on one device may be relied on, other than what follows from the above.
Results may differ from the reference program's by a relative error of at most 0.0003.
The reference program's roundings to bfloat16 on the way (of `stats`) count: a program that leaves them out, or rounds other values in their place, can miss the bound.
Values may be sent and summed in bfloat16 or wider, within the bound.
No kernel may reach another device: no remote copies, remote signals or barrier semaphores. Data moves between devices by JAX's collectives and lax.ppermute only.
A program may use at most 64 MiB of HBM per device.

```python
import jax
import jax.numpy as jnp
from jax import lax

F = 512
BINS = 256
NODES = 8
TIE_MOST = 8
ROWS = 131072


def draw_tie_groups(key, part):
    row_index = jnp.arange(ROWS, dtype=jnp.int32)
    coin_flips = jax.random.randint(key, (ROWS,), 0, 3)
    begins = (coin_flips == 0) | (row_index % TIE_MOST == 0)
    begins = jnp.where(row_index < TIE_MOST, row_index == 0, begins)
    finish = jnp.concatenate([begins[1:], jnp.ones((1,), jnp.bool_)])
    return lax.cummin(jnp.where(finish, row_index, ROWS - 1), axis=0, reverse=True).astype(jnp.int32)


def set_ends(entries, stream_key, least, largest):
    shape = entries.shape
    place = [jax.random.randint(jax.random.fold_in(stream_key, axis), (), 0, shape[axis]) for axis in range(len(shape))]
    entries = entries.at[tuple(place)].set(least)
    longest = shape.index(max(shape))
    place[longest] = (place[longest] + 1) % shape[longest]
    return entries.at[tuple(place)].set(largest)


def level_of(stream_key, shape, shards, low, top_value):
    def one(position, blocks):
        steps = jax.random.uniform(jax.random.fold_in(jax.random.fold_in(stream_key, 6), position), (blocks,), jnp.float32, low / len(shards), top_value / len(shards))
        return jnp.repeat(jnp.exp(steps), shape[position] // blocks).reshape((-1,) + (1,) * (len(shape) - position - 1))

    level = one(*shards[0])
    for cut in shards[1:]:
        level = level * one(*cut)
    return level


def scatter_about(own_key, dims, scale, most, split=(), kind=jnp.bfloat16):
    drawn = scale * jax.random.normal(own_key, dims, jnp.float32)
    if split:
        drawn = drawn * level_of(own_key, dims, split, -0.22, 0.18)
    return jnp.clip(drawn, -most, most).astype(kind)


def setup_inputs(seed: int = 0) -> dict:
    seeds = jax.random.split(jax.random.key(seed), 6)
    predictor = scatter_about(seeds[0], (ROWS,), 0.5, 3.0, ((0, 256),), jnp.float32)
    events = set_ends((jax.random.randint(seeds[1], (ROWS,), 0, 2) < 1).astype(jnp.int32), jax.random.fold_in(seeds[1], 1), 0, 1)
    tie_groups = draw_tie_groups(jax.random.fold_in(seeds[5], 71), 0)
    node_ids = set_ends(jax.random.randint(seeds[3], (ROWS,), 0, NODES), jax.random.fold_in(seeds[3], 1), 0, NODES - 1).astype(jnp.int32)
    bin_index = set_ends(jax.random.randint(seeds[4], (F, ROWS), 0, BINS), jax.random.fold_in(seeds[4], 1), 0, BINS - 1).astype(jnp.int32)
    return {"predictor": predictor, "events": events, "tie_groups": tie_groups, "node_ids": node_ids, "bin_index": bin_index}


def group_bounds(tie_groups):
    length = tie_groups.shape[0]
    row_index = jnp.arange(length, dtype=jnp.int32)
    change = tie_groups[1:] != tie_groups[:-1]
    begins = jnp.concatenate([jnp.ones((1,), jnp.bool_), change])
    finish = jnp.concatenate([change, jnp.ones((1,), jnp.bool_)])
    first_row = lax.cummax(jnp.where(begins, row_index, 0), axis=0)
    last_row = lax.cummin(jnp.where(finish, row_index, length - 1), axis=0, reverse=True)
    return first_row, last_row


def reference(predictor, events, tie_groups, node_ids, bin_index):
    hazard_exp = jnp.exp(predictor)
    suffix = jnp.cumsum(hazard_exp[::-1])[::-1]
    first_row, last_row = group_bounds(tie_groups)
    risk_sum = suffix[first_row]
    failed = events.astype(jnp.float32)
    weight_one = failed / risk_sum
    weight_two = failed / (risk_sum * risk_sum)
    hazard_one = jnp.cumsum(weight_one)[last_row]
    hazard_two = jnp.cumsum(weight_two)[last_row]
    gradient = hazard_exp * hazard_one - failed
    hessian = hazard_exp * hazard_one - hazard_exp * hazard_exp * hazard_two
    rounded = lax.optimization_barrier(jnp.stack([gradient, hessian]).astype(jnp.bfloat16))
    stats = rounded.astype(jnp.float32).T

    def feature_hist(column):
        segment = node_ids * BINS + column
        summed = jax.ops.segment_sum(stats, segment, num_segments=NODES * BINS)
        return summed.reshape(NODES, BINS, 2).transpose(0, 2, 1)

    hist = lax.map(feature_hist, bin_index)
    left_sums = jnp.cumsum(hist, axis=3)
    totals = jnp.sum(hist, axis=3, keepdims=True)
    grad_left = left_sums[:, :, 0]
    hess_left = left_sums[:, :, 1]
    grad_all = totals[:, :, 0]
    hess_all = totals[:, :, 1]
    gain = (grad_left * grad_left / (hess_left + 1.0)
            + (grad_all - grad_left) ** 2 / (hess_all - hess_left + 1.0)
            - grad_all * grad_all / (hess_all + 1.0))
    return gradient, hessian, gain.transpose(1, 0, 2)
```

```python
import jax
import jax.numpy as jnp
from jax import lax
from jax.experimental import pallas as pl
from jax.experimental.pallas import tpu as pltpu
from jax.sharding import Mesh
from jax.sharding import PartitionSpec as P

NODES = 8
LANES = 128
FEAT = ("feat_0", "feat_1")
ROW = ("row_0", "row_1")
ROW_FEAT = ROW + FEAT
BF = jnp.bfloat16
F32 = jnp.float32
FAR = 1e30
CHUNK = 512
GROUP = 2


def iota(shape, dim):
    return lax.broadcasted_iota(jnp.int32, shape, dim)


def thirds(x):
    first = x.astype(BF)
    left = x - first.astype(F32)
    second = left.astype(BF)
    third = (left - second.astype(F32)).astype(BF)
    return first, second, third


def times_right(x, ones):
    rows = x.shape[0]
    y = jnp.dot(jnp.concatenate(thirds(x), 0), ones, preferred_element_type=F32)
    return y[:rows] + y[rows : 2 * rows] + y[2 * rows :]


def times_left(ones, x):
    width = x.shape[1]
    y = jnp.dot(ones, jnp.concatenate(thirds(x), 1), preferred_element_type=F32)
    return y[:, :width] + y[:, width : 2 * width] + y[:, 2 * width :]


def as_ones(mask):
    return jnp.where(mask, 1.0, 0.0).astype(BF)


def spread_kernel(pred_ref, ev_ref, tie_ref, out_ref):
    three = jnp.concatenate(
        [pred_ref[...], ev_ref[...].astype(F32), tie_ref[...].astype(F32)], 0
    )
    for k in range(out_ref.shape[0]):
        out_ref[k] = three


def risk_kernel(got_ref, msg_ref, own_ref):
    blocks, quarter = got_ref.shape[0], got_ref.shape[1] // 3
    rows = blocks * quarter
    for k in range(blocks):
        for j in range(3):
            own_ref[j, k * quarter : (k + 1) * quarter, :] = got_ref[
                k, j * quarter : (j + 1) * quarter, :
            ]
    hazard = jnp.exp(own_ref[0])
    tie = own_ref[2]
    own_ref[0] = hazard
    lanes = (LANES, LANES)
    inside = times_right(hazard, as_ones(iota(lanes, 0) >= iota(lanes, 1)))
    totals = jnp.broadcast_to(inside[:, 0:1], inside.shape)
    square = (rows, rows)
    suffix = inside + times_left(as_ones(iota(square, 1) > iota(square, 0)), totals)
    place = iota((rows, LANES), 1) % 8
    first = suffix
    for k in (1, 2, 4):
        same = (pltpu.roll(tie, k, 1) == tie) & (place >= k)
        first = jnp.where(same, pltpu.roll(first, k, 1), first)
    own_ref[3] = first
    value = jnp.where(own_ref[1] > 0.5, first, FAR)
    total = jnp.broadcast_to(suffix[0:1, 0:1], (8, LANES))
    for k in range(msg_ref.shape[0]):
        msg_ref[k, 0:rows, :] = value
        msg_ref[k, rows : rows + 8, :] = total


def hist_kernel(
    got_ref, own_ref, node_ref, hi_ref, lo_ref,
    grad_ref, hess_ref, out_ref, grad_buf, hess_buf, stat_buf,
):
    shards, rows = got_ref.shape[0], own_ref.shape[1]
    row, feat = lax.axis_index(ROW), lax.axis_index(FEAT)
    later = own_later = jnp.zeros((1, LANES), F32)
    sum_one = sum_two = jnp.zeros((rows, LANES), F32)
    for k in reversed(range(shards)):
        value = got_ref[k, 0:rows, :]
        total = got_ref[k, rows : rows + 1, :]
        weight = jnp.where((value < FAR * 0.1) & (k < row), 1.0 / (value + later), 0.0)
        sum_one += weight
        sum_two += weight * weight
        own_later = jnp.where(k > row, own_later + total, own_later)
        later += total

    def whole(x):
        return jnp.sum(jnp.sum(x, 0, keepdims=True), 1, keepdims=True)

    hazard, failed, tie = own_ref[0], own_ref[1], own_ref[2]
    risk = own_ref[3] + own_later
    one = failed / risk
    both = jnp.concatenate([one, failed / (risk * risk)], 0)
    lanes = (LANES, LANES)
    inside = times_right(both, as_ones(iota(lanes, 0) <= iota(lanes, 1)))
    totals = jnp.broadcast_to(inside[:, LANES - 1 : LANES], inside.shape)
    square = (2 * rows, 2 * rows)
    earlier = (iota(square, 1) < iota(square, 0)) & (
        iota(square, 1) // rows == iota(square, 0) // rows
    )
    upto = inside + times_left(as_ones(earlier), totals)
    haz_one = upto[:rows] + whole(sum_one)
    haz_two = upto[rows:] + whole(sum_two)
    place = iota((rows, LANES), 1) % 8
    for k in (1, 2, 4):
        same = (pltpu.roll(tie, LANES - k, 1) == tie) & (place < 8 - k)
        haz_one = jnp.where(same, pltpu.roll(haz_one, LANES - k, 1), haz_one)
        haz_two = jnp.where(same, pltpu.roll(haz_two, LANES - k, 1), haz_two)
    gradient = hazard * haz_one - failed
    hessian = hazard * haz_one - hazard * hazard * haz_two
    grad_buf[...] = gradient
    hess_buf[...] = hessian
    quarter = grad_ref.shape[0]
    grad_ref[...] = grad_buf[pl.ds(feat * quarter, quarter), :]
    hess_ref[...] = hess_buf[pl.ds(feat * quarter, quarter), :]

    levels = iota((NODES, LANES), 0)
    for k in range(rows):
        here = node_ref[k : k + 1, :] == levels
        stat = jnp.concatenate(
            [
                jnp.where(here, gradient[k : k + 1, :], 0.0),
                jnp.where(here, hessian[k : k + 1, :], 0.0),
            ],
            0,
        )
        stat_buf[:, k * LANES : (k + 1) * LANES] = stat.astype(BF)

    feats, length = hi_ref.shape
    tops = iota((shards, CHUNK), 0).astype(F32).astype(BF)
    zero, unit = jnp.zeros((), BF), jnp.ones((), BF)

    def some_features(g, _):
        acc = None
        for c in range(length // CHUNK):
            cols = pl.ds(c * CHUNK, CHUNK)
            stat = stat_buf[:, cols]
            tall, wide = [], []
            for j in range(GROUP):
                at = pl.ds(g * GROUP + j, 1)
                lo = jnp.broadcast_to(lo_ref[at, cols], (2 * NODES, CHUNK)).astype(BF)
                hi = jnp.broadcast_to(hi_ref[at, cols], (2 * NODES, CHUNK)).astype(BF)
                hi = jnp.concatenate([hi, hi], 0)
                tall.append(jnp.where(hi == tops, unit, zero))
                for b in range(7):
                    wide.append(jnp.where(lo <= jnp.asarray(b, BF), stat, zero))
                wide.append(stat)
            part = lax.dot_general(
                jnp.concatenate(tall, 0), jnp.concatenate(wide, 0),
                (((1,), (1,)), ((), ())), preferred_element_type=F32,
            )
            acc = part if acc is None else acc + part
        for j in range(GROUP):
            out_ref[:, g * GROUP + j, :] = acc[
                shards * j : shards * (j + 1), LANES * j : LANES * (j + 1)
            ]
        return 0

    lax.fori_loop(0, feats // GROUP, some_features, 0)

    last = iota((8, LANES), 1) >= LANES - 2 * NODES

    def eight_features(g, _):
        at = pl.ds(pl.multiple_of(g * 8, 8), 8)
        below = jnp.zeros((8, LANES), F32)
        for k in range(shards):
            block = out_ref[k, at, :]
            out_ref[k, at, :] = block + below
            step = jnp.where(last, block, 0.0)
            for shift in (64, 32, 16):
                step += pltpu.roll(step, shift, 1)
            below += step
        return 0

    lax.fori_loop(0, feats // 8, eight_features, 0)
    final = out_ref[shards - 1, 0:8, :]
    for k in range(shards):
        out_ref[k, feats : feats + 8, :] = final


def gain_kernel(got_ref, out_ref):
    shards, feats = got_ref.shape[0], got_ref.shape[1] - 8
    left = got_ref[0]
    for k in range(1, shards):
        left += got_ref[k]
    total = left[feats : feats + 1, :]
    left = left[:feats]
    total = jnp.where(iota((1, LANES), 1) >= LANES - 2 * NODES, total, 0.0)
    for shift in (64, 32, 16):
        total += pltpu.roll(total, shift, 1)
    grad, hess = left, pltpu.roll(left, LANES - NODES, 1)
    grad_all, hess_all = total, pltpu.roll(total, LANES - NODES, 1)
    gain = (
        grad * grad / (hess + 1.0)
        + (grad_all - grad) * (grad_all - grad) / (hess_all - hess + 1.0)
        - grad_all * grad_all / (hess_all + 1.0)
    )
    gain = jnp.where(iota(gain.shape, 1) % (2 * NODES) < NODES, gain, 0.0)
    shape = (NODES * 8, LANES)
    spot, lane = iota(shape, 0), iota(shape, 1)
    chosen = as_ones(lane == (spot % 8) * 2 * NODES + spot // 8)
    turned = None
    for part in thirds(gain):
        one = lax.dot_general(
            chosen, part, (((1,), (1,)), ((), ())), preferred_element_type=F32
        )
        turned = one if turned is None else turned + one
    for n in range(NODES):
        out_ref[n] = turned[n * 8 : (n + 1) * 8, :]


def call(kernel, outs, n_in, name, scratch=()):
    vmem = pl.BlockSpec(memory_space=pltpu.VMEM)
    return pl.pallas_call(
        kernel,
        out_shape=outs,
        in_specs=[vmem] * n_in,
        out_specs=jax.tree.map(lambda _: vmem, outs),
        scratch_shapes=scratch,
        compiler_params=pltpu.CompilerParams(vmem_limit_bytes=48 << 20),
        name=name,
    )


def exchange(blocks, axes):
    return lax.all_to_all(blocks, axes, 0, 0, tiled=True)


def shards(predictor, events, tie_groups, node_ids, bin_index):
    shape = jax.ShapeDtypeStruct
    n_row, n_feat = lax.axis_size(ROW), lax.axis_size(FEAT)
    quarter = predictor.shape[0] // LANES
    rows = quarter * n_feat
    feats, length = bin_index.shape
    lines = [a.reshape(quarter, LANES) for a in (predictor, events, tie_groups)]
    spread = call(spread_kernel, shape((n_feat, 3 * quarter, LANES), F32), 3, "spread")(*lines)
    got = exchange(spread, FEAT)
    message, own = call(
        risk_kernel,
        (shape((n_row, rows + 8, LANES), F32), shape((4, rows, LANES), F32)),
        1,
        "risk",
    )(got)
    received = exchange(message, ROW)
    hi = (bin_index // 8).astype(F32)
    lo = (bin_index % 8).astype(F32)
    gradient, hessian, left = call(
        hist_kernel,
        (
            shape((quarter, LANES), F32),
            shape((quarter, LANES), F32),
            shape((n_row, feats + 8, LANES), F32),
        ),
        5,
        "hist",
        (
            pltpu.VMEM((rows, LANES), F32),
            pltpu.VMEM((rows, LANES), F32),
            pltpu.VMEM((2 * NODES, length), BF),
        ),
    )(received, own, node_ids.reshape(rows, LANES), hi, lo)
    summed = exchange(left, ROW)
    gain = call(gain_kernel, shape((NODES, 8, feats), F32), 1, "gain")(summed)
    return gradient.reshape(-1), hessian.reshape(-1), gain.transpose(0, 2, 1)


def solution(mesh):
    finer = Mesh(mesh.devices.reshape(4, 8, 4, 2), ROW_FEAT)
    in_specs = (P(ROW_FEAT), P(ROW_FEAT), P(ROW_FEAT), P(ROW), P(FEAT, ROW))
    out_specs = (P(ROW_FEAT), P(ROW_FEAT), P(None, FEAT, ROW))
    return jax.shard_map(
        shards, mesh=finer, in_specs=in_specs, out_specs=out_specs, check_vma=False
    )
```

```python
import jax
import jax.numpy as jnp
from jax import lax
from jax.experimental import pallas as pl
from jax.experimental.pallas import tpu as pltpu
from jax.sharding import Mesh
from jax.sharding import PartitionSpec as P

NODES = 8
LANES = 128
FEAT = ("feat_0", "feat_1")
ROW = ("row_0", "row_1")
ROW_FEAT = ROW + FEAT
BF = jnp.bfloat16
F32 = jnp.float32
CHUNK = 512
GROUP = 2
UNROLL = 4


def iota(shape, dim):
    return lax.broadcasted_iota(jnp.int32, shape, dim)


def thirds(x):
    first = x.astype(BF)
    left = x - first.astype(F32)
    second = left.astype(BF)
    third = (left - second.astype(F32)).astype(BF)
    return first, second, third


def times_right(x, ones):
    rows = x.shape[0]
    y = jnp.dot(jnp.concatenate(thirds(x), 0), ones, preferred_element_type=F32)
    return y[:rows] + y[rows : 2 * rows] + y[2 * rows :]


def times_left(ones, x):
    width = x.shape[1]
    y = jnp.dot(ones, jnp.concatenate(thirds(x), 1), preferred_element_type=F32)
    return y[:, :width] + y[:, width : 2 * width] + y[:, 2 * width :]


def as_ones(mask):
    return jnp.where(mask, 1.0, 0.0).astype(BF)


def spread_kernel(pred_ref, ev_ref, tie_ref, out_ref, pred, ev, tie, sems):
    copies = [
        pltpu.make_async_copy(source, target, sems.at[k])
        for k, (source, target) in enumerate(
            ((pred_ref, pred), (ev_ref, ev), (tie_ref, tie))
        )
    ]
    for copy in copies:
        copy.start()
    for copy in copies:
        copy.wait()
    three = jnp.concatenate(
        [pred[...], ev[...].astype(F32), tie[...].astype(F32)], 0
    )
    for k in range(out_ref.shape[0]):
        out_ref[k] = three


def risk_kernel(got_ref, msg_ref, own_ref):
    blocks, quarter = got_ref.shape[0], got_ref.shape[1] // 3
    rows = blocks * quarter
    for k in range(blocks):
        for j in range(3):
            own_ref[j, k * quarter : (k + 1) * quarter, :] = got_ref[
                k, j * quarter : (j + 1) * quarter, :
            ]
    hazard = jnp.exp(own_ref[0])
    tie = own_ref[2]
    own_ref[0] = hazard
    lanes = (LANES, LANES)
    inside = times_right(hazard, as_ones(iota(lanes, 0) >= iota(lanes, 1)))
    totals = jnp.broadcast_to(inside[:, 0:1], inside.shape)
    square = (rows, rows)
    suffix = inside + times_left(as_ones(iota(square, 1) > iota(square, 0)), totals)
    place = iota((rows, LANES), 1) % 8
    first = suffix
    for k in (1, 2, 4):
        same = (pltpu.roll(tie, k, 1) == tie) & (place >= k)
        first = jnp.where(same, pltpu.roll(first, k, 1), first)
    own_ref[3] = first
    signed = jnp.where(own_ref[1] > 0.5, first, -first)
    for k in range(msg_ref.shape[0]):
        msg_ref[k] = signed


def hist_kernel(
    got_ref, own_ref, node_ref, hi_ref, lo_ref,
    grad_ref, hess_ref, out_ref, grad_buf, hess_buf, stat_buf, node_buf,
):
    shards, rows = got_ref.shape[0], own_ref.shape[1]
    row, feat = lax.axis_index(ROW), lax.axis_index(FEAT)
    later = own_later = jnp.zeros((1, LANES), F32)
    sum_one = sum_two = jnp.zeros((rows, LANES), F32)
    for k in reversed(range(shards)):
        value = got_ref[k]
        total = jnp.broadcast_to(jnp.abs(value[0:1, 0:1]), (1, LANES))
        weight = jnp.where((value > 0.0) & (k < row), 1.0 / (value + later), 0.0)
        sum_one += weight
        sum_two += weight * weight
        own_later = jnp.where(k > row, own_later + total, own_later)
        later += total

    def whole(x):
        return jnp.sum(jnp.sum(x, 0, keepdims=True), 1, keepdims=True)

    hazard, failed, tie = own_ref[0], own_ref[1], own_ref[2]
    risk = own_ref[3] + own_later
    one = failed / risk
    both = jnp.concatenate([one, failed / (risk * risk)], 0)
    lanes = (LANES, LANES)
    inside = times_right(both, as_ones(iota(lanes, 0) <= iota(lanes, 1)))
    totals = jnp.broadcast_to(inside[:, LANES - 1 : LANES], inside.shape)
    square = (2 * rows, 2 * rows)
    earlier = (iota(square, 1) < iota(square, 0)) & (
        iota(square, 1) // rows == iota(square, 0) // rows
    )
    upto = inside + times_left(as_ones(earlier), totals)
    haz_one = upto[:rows] + whole(sum_one)
    haz_two = upto[rows:] + whole(sum_two)
    place = iota((rows, LANES), 1) % 8
    for k in (1, 2, 4):
        same = (pltpu.roll(tie, LANES - k, 1) == tie) & (place < 8 - k)
        haz_one = jnp.where(same, pltpu.roll(haz_one, LANES - k, 1), haz_one)
        haz_two = jnp.where(same, pltpu.roll(haz_two, LANES - k, 1), haz_two)
    gradient = hazard * haz_one - failed
    hessian = hazard * haz_one - hazard * hazard * haz_two
    grad_buf[...] = gradient
    hess_buf[...] = hessian
    quarter = grad_ref.shape[0]
    grad_ref[...] = grad_buf[pl.ds(feat * quarter, quarter), :]
    hess_ref[...] = hess_buf[pl.ds(feat * quarter, quarter), :]

    wide = (2 * NODES, LANES)
    levels = iota(wide, 0) % NODES
    for k in range(rows):
        cols = slice(k * LANES, (k + 1) * LANES)
        node_buf[:, cols] = as_ones(node_ref[k : k + 1, :] == levels)
        for j, stat in enumerate((gradient, hessian)):
            stat_buf[j, :, cols] = jnp.broadcast_to(stat[k : k + 1, :], wide).astype(BF)

    feats, length = hi_ref.shape
    tops = iota((shards, CHUNK), 0).astype(F32).astype(BF)
    bins = (iota((8 * NODES, CHUNK), 0) // NODES).astype(F32).astype(BF)
    zero = jnp.zeros((), BF)
    half = iota((shards, LANES), 1) < LANES // 2

    def some_features(g, _):
        acc = None
        for c in range(length // CHUNK):
            cols = pl.ds(c * CHUNK, CHUNK)
            node = jnp.concatenate([node_buf[:, cols]] * 4, 0)
            grad = jnp.concatenate([stat_buf[0, :, cols]] * 2, 0)
            hess = jnp.concatenate([stat_buf[1, :, cols]] * 2, 0)
            upper, lower = [], []
            for j in range(GROUP):
                at = pl.ds(g * GROUP + j, 1)
                lo = jnp.broadcast_to(lo_ref[at, cols], (2 * NODES, CHUNK)).astype(BF)
                hi = jnp.broadcast_to(hi_ref[at, cols], (2 * NODES, CHUNK)).astype(BF)
                top = jnp.concatenate([hi] * 2, 0) == tops
                upper += [jnp.where(top, grad, zero), jnp.where(top, hess, zero)]
                reached = jnp.concatenate([lo] * 4, 0) <= bins
                lower.append(jnp.where(reached, node, zero))
            part = lax.dot_general(
                jnp.concatenate(upper, 0), jnp.concatenate(lower, 0),
                (((1,), (1,)), ((), ())), preferred_element_type=F32,
            )
            acc = part if acc is None else acc + part
        for j in range(GROUP):
            rows_of = slice(2 * shards * j, 2 * shards * (j + 1))
            lanes_of = slice(LANES * (j // 2), LANES * (j // 2 + 1))
            both = acc[rows_of, lanes_of]
            grad, hess = both[:shards], both[shards:]
            if j % 2 == 0:
                hess = pltpu.roll(hess, LANES // 2, 1)
            else:
                grad = pltpu.roll(grad, LANES // 2, 1)
            out_ref[:, g * GROUP + j, :] = jnp.where(half, grad, hess)
        return 0

    lax.fori_loop(0, feats // GROUP, some_features, 0, unroll=UNROLL)

    last = iota((8, LANES), 1) % (LANES // 2) >= LANES // 2 - NODES

    def eight_features(g, _):
        at = pl.ds(pl.multiple_of(g * 8, 8), 8)
        below = jnp.zeros((8, LANES), F32)
        for k in range(shards):
            block = out_ref[k, at, :]
            out_ref[k, at, :] = block + below
            step = jnp.where(last, block, 0.0)
            for shift in (32, 16, 8):
                step += pltpu.roll(step, LANES - shift, 1)
            below += step
        return 0

    lax.fori_loop(0, feats // 8, eight_features, 0)
    final = out_ref[shards - 1, 0:8, :]
    for k in range(shards):
        out_ref[k, feats : feats + 8, :] = final


def gain_kernel(got_ref, out_ref):
    shards, feats = got_ref.shape[0], got_ref.shape[1] - 8
    left = got_ref[0]
    for k in range(1, shards):
        left += got_ref[k]
    total = left[feats : feats + 1, :]
    left = left[:feats]
    last = iota((1, LANES), 1) % (LANES // 2) >= LANES // 2 - NODES
    total = jnp.where(last, total, 0.0)
    for shift in (32, 16, 8):
        total += pltpu.roll(total, LANES - shift, 1)
    grad, hess = left, pltpu.roll(left, LANES // 2, 1)
    grad_all, hess_all = total, pltpu.roll(total, LANES // 2, 1)
    gain = (
        grad * grad / (hess + 1.0)
        + (grad_all - grad) * (grad_all - grad) / (hess_all - hess + 1.0)
        - grad_all * grad_all / (hess_all + 1.0)
    )
    gain = jnp.where(iota(gain.shape, 1) < LANES // 2, gain, 0.0)
    shape = (NODES * 8, LANES)
    spot, lane = iota(shape, 0), iota(shape, 1)
    chosen = as_ones(lane == (spot % 8) * NODES + spot // 8)
    turned = None
    for part in thirds(gain):
        one = lax.dot_general(
            chosen, part, (((1,), (1,)), ((), ())), preferred_element_type=F32
        )
        turned = one if turned is None else turned + one
    for n in range(NODES):
        out_ref[n] = turned[n * 8 : (n + 1) * 8, :]


def call(kernel, outs, n_in, name, scratch=(), space=pltpu.VMEM):
    vmem = pl.BlockSpec(memory_space=pltpu.VMEM)
    return pl.pallas_call(
        kernel,
        out_shape=outs,
        in_specs=[pl.BlockSpec(memory_space=space)] * n_in,
        out_specs=jax.tree.map(lambda _: vmem, outs),
        scratch_shapes=scratch,
        compiler_params=pltpu.CompilerParams(vmem_limit_bytes=48 << 20),
        name=name,
    )


def exchange(blocks, axes):
    return lax.all_to_all(blocks, axes, 0, 0, tiled=True)


def shards(predictor, events, tie_groups, node_ids, bin_index):
    shape = jax.ShapeDtypeStruct
    n_row, n_feat = lax.axis_size(ROW), lax.axis_size(FEAT)
    quarter = predictor.shape[0] // LANES
    rows = quarter * n_feat
    feats, length = bin_index.shape
    lines = [a.reshape(quarter, LANES) for a in (predictor, events, tie_groups)]
    spread = call(
        spread_kernel,
        shape((n_feat, 3 * quarter, LANES), F32),
        3,
        "spread",
        [pltpu.VMEM(a.shape, a.dtype) for a in lines] + [pltpu.SemaphoreType.DMA((3,))],
        pltpu.HBM,
    )(*lines)
    got = exchange(spread, FEAT)
    message, own = call(
        risk_kernel,
        (shape((n_row, rows, LANES), F32), shape((4, rows, LANES), F32)),
        1,
        "risk",
    )(got)
    received = exchange(message, ROW)
    hi = (bin_index // 8).astype(F32)
    lo = (bin_index % 8).astype(F32)
    gradient, hessian, left = call(
        hist_kernel,
        (
            shape((quarter, LANES), F32),
            shape((quarter, LANES), F32),
            shape((n_row, feats + 8, LANES), F32),
        ),
        5,
        "hist",
        (
            pltpu.VMEM((rows, LANES), F32),
            pltpu.VMEM((rows, LANES), F32),
            pltpu.VMEM((2, 2 * NODES, length), BF),
            pltpu.VMEM((2 * NODES, length), BF),
        ),
    )(received, own, node_ids.reshape(rows, LANES), hi, lo)
    summed = exchange(left, ROW)
    gain = call(gain_kernel, shape((NODES, 8, feats), F32), 1, "gain")(summed)
    return gradient.reshape(-1), hessian.reshape(-1), gain.transpose(0, 2, 1)


def solution(mesh):
    finer = Mesh(mesh.devices.reshape(4, 8, 4, 2), ROW_FEAT)
    in_specs = (P(ROW_FEAT), P(ROW_FEAT), P(ROW_FEAT), P(ROW), P(FEAT, ROW))
    out_specs = (P(ROW_FEAT), P(ROW_FEAT), P(None, FEAT, ROW))
    return jax.shard_map(
        shards, mesh=finer, in_specs=in_specs, out_specs=out_specs, check_vma=False
    )
```

```python
import jax
import jax.numpy as jnp
from jax import lax
from jax.experimental import pallas as pl
from jax.experimental.pallas import tpu as pltpu
from jax.sharding import Mesh
from jax.sharding import PartitionSpec as P

NODES = 8
LANES = 128
FEAT = ("feat_0", "feat_1")
ROW = ("row_0", "row_1")
ROW_FEAT = ROW + FEAT
BF = jnp.bfloat16
F32 = jnp.float32
CHUNK = 512
GROUP = 2
UNROLL = 4


def iota(shape, dim):
    return lax.broadcasted_iota(jnp.int32, shape, dim)


def thirds(x):
    first = x.astype(BF)
    left = x - first.astype(F32)
    second = left.astype(BF)
    third = (left - second.astype(F32)).astype(BF)
    return first, second, third


def times_right(x, ones):
    rows = x.shape[0]
    y = jnp.dot(jnp.concatenate(thirds(x), 0), ones, preferred_element_type=F32)
    return y[:rows] + y[rows : 2 * rows] + y[2 * rows :]


def times_left(ones, x):
    width = x.shape[1]
    y = jnp.dot(ones, jnp.concatenate(thirds(x), 1), preferred_element_type=F32)
    return y[:, :width] + y[:, width : 2 * width] + y[:, 2 * width :]


def as_ones(mask):
    return jnp.where(mask, 1.0, 0.0).astype(BF)


def spread_kernel(pred_ref, ev_ref, tie_ref, out_ref, pred, ev, tie, sems):
    copies = [
        pltpu.make_async_copy(source, target, sems.at[k])
        for k, (source, target) in enumerate(
            ((pred_ref, pred), (ev_ref, ev), (tie_ref, tie))
        )
    ]
    for copy in copies:
        copy.start()
    for copy in copies:
        copy.wait()
    three = jnp.concatenate(
        [pred[...], ev[...].astype(F32), tie[...].astype(F32)], 0
    )
    for k in range(out_ref.shape[0]):
        out_ref[k] = three


def risk_kernel(got_ref, msg_ref, own_ref):
    blocks, quarter = got_ref.shape[0], got_ref.shape[1] // 3
    rows = blocks * quarter
    for k in range(blocks):
        for j in range(3):
            own_ref[j, k * quarter : (k + 1) * quarter, :] = got_ref[
                k, j * quarter : (j + 1) * quarter, :
            ]
    hazard = jnp.exp(own_ref[0])
    tie = own_ref[2]
    own_ref[0] = hazard
    lanes = (LANES, LANES)
    inside = times_right(hazard, as_ones(iota(lanes, 0) >= iota(lanes, 1)))
    totals = jnp.broadcast_to(inside[:, 0:1], inside.shape)
    square = (rows, rows)
    suffix = inside + times_left(as_ones(iota(square, 1) > iota(square, 0)), totals)
    place = iota((rows, LANES), 1) % 8
    first = suffix
    for k in (1, 2, 4):
        same = (pltpu.roll(tie, k, 1) == tie) & (place >= k)
        first = jnp.where(same, pltpu.roll(first, k, 1), first)
    own_ref[3] = first
    signed = jnp.where(own_ref[1] > 0.5, first, -first)
    for k in range(msg_ref.shape[0]):
        msg_ref[k] = signed


def hist_kernel(
    got_ref, own_ref, node_ref, hi_ref, lo_ref,
    grad_ref, hess_ref, out_ref, grad_buf, hess_buf, stat_buf, node_buf, sums_buf,
):
    shards, rows = got_ref.shape[0], own_ref.shape[1]
    row, feat = lax.axis_index(ROW), lax.axis_index(FEAT)
    later = own_later = jnp.zeros((1, LANES), F32)
    sum_one = sum_two = jnp.zeros((rows, LANES), F32)
    for k in reversed(range(shards)):
        value = got_ref[k]
        total = jnp.broadcast_to(jnp.abs(value[0:1, 0:1]), (1, LANES))
        weight = jnp.where((value > 0.0) & (k < row), 1.0 / (value + later), 0.0)
        sum_one += weight
        sum_two += weight * weight
        own_later = jnp.where(k > row, own_later + total, own_later)
        later += total

    def whole(x):
        return jnp.sum(jnp.sum(x, 0, keepdims=True), 1, keepdims=True)

    hazard, failed, tie = own_ref[0], own_ref[1], own_ref[2]
    risk = own_ref[3] + own_later
    one = failed / risk
    both = jnp.concatenate([one, failed / (risk * risk)], 0)
    lanes = (LANES, LANES)
    inside = times_right(both, as_ones(iota(lanes, 0) <= iota(lanes, 1)))
    totals = jnp.broadcast_to(inside[:, LANES - 1 : LANES], inside.shape)
    square = (2 * rows, 2 * rows)
    earlier = (iota(square, 1) < iota(square, 0)) & (
        iota(square, 1) // rows == iota(square, 0) // rows
    )
    upto = inside + times_left(as_ones(earlier), totals)
    haz_one = upto[:rows] + whole(sum_one)
    haz_two = upto[rows:] + whole(sum_two)
    place = iota((rows, LANES), 1) % 8
    for k in (1, 2, 4):
        same = (pltpu.roll(tie, LANES - k, 1) == tie) & (place < 8 - k)
        haz_one = jnp.where(same, pltpu.roll(haz_one, LANES - k, 1), haz_one)
        haz_two = jnp.where(same, pltpu.roll(haz_two, LANES - k, 1), haz_two)
    gradient = hazard * haz_one - failed
    hessian = hazard * haz_one - hazard * hazard * haz_two
    grad_buf[...] = gradient
    hess_buf[...] = hessian
    quarter = grad_ref.shape[0]
    grad_ref[...] = grad_buf[pl.ds(feat * quarter, quarter), :]
    hess_ref[...] = hess_buf[pl.ds(feat * quarter, quarter), :]

    wide = (2 * NODES, LANES)
    levels = iota(wide, 0) % NODES
    for k in range(rows):
        cols = slice(k * LANES, (k + 1) * LANES)
        node_buf[:, cols] = as_ones(node_ref[k : k + 1, :] == levels)
        for j, stat in enumerate((gradient, hessian)):
            stat_buf[j, :, cols] = jnp.broadcast_to(stat[k : k + 1, :], wide).astype(BF)

    feats, length = hi_ref.shape
    tops = iota((shards, CHUNK), 0).astype(F32).astype(BF)
    bins = (iota((8 * NODES, CHUNK), 0) // NODES).astype(F32).astype(BF)
    zero = jnp.zeros((), BF)
    half = iota((shards, LANES), 1) < LANES // 2

    def some_features(g, _):
        acc = None
        for c in range(length // CHUNK):
            cols = pl.ds(c * CHUNK, CHUNK)
            node = jnp.concatenate([node_buf[:, cols]] * 4, 0)
            grad = jnp.concatenate([stat_buf[0, :, cols]] * 2, 0)
            hess = jnp.concatenate([stat_buf[1, :, cols]] * 2, 0)
            upper, lower = [], []
            for j in range(GROUP):
                at = pl.ds(g * GROUP + j, 1)
                lo = jnp.broadcast_to(lo_ref[at, cols], (2 * NODES, CHUNK)).astype(BF)
                hi = jnp.broadcast_to(hi_ref[at, cols], (2 * NODES, CHUNK)).astype(BF)
                top = jnp.concatenate([hi] * 2, 0) == tops
                upper += [jnp.where(top, grad, zero), jnp.where(top, hess, zero)]
                reached = jnp.concatenate([lo] * 4, 0) <= bins
                lower.append(jnp.where(reached, node, zero))
            part = lax.dot_general(
                jnp.concatenate(upper, 0), jnp.concatenate(lower, 0),
                (((1,), (1,)), ((), ())), preferred_element_type=F32,
            )
            acc = part if acc is None else acc + part
        for j in range(GROUP):
            rows_of = slice(2 * shards * j, 2 * shards * (j + 1))
            lanes_of = slice(LANES * (j // 2), LANES * (j // 2 + 1))
            both = acc[rows_of, lanes_of]
            grad, hess = both[:shards], both[shards:]
            if j % 2 == 0:
                hess = pltpu.roll(hess, LANES // 2, 1)
            else:
                grad = pltpu.roll(grad, LANES // 2, 1)
            sums_buf[:, g * GROUP + j, :] = jnp.where(half, grad, hess)
        return 0

    last = iota((8, LANES), 1) % (LANES // 2) >= LANES // 2 - NODES

    def eight_features(g, _):
        at = pl.ds(pl.multiple_of(g * 8, 8), 8)
        below = jnp.zeros((8, LANES), F32)
        for k in range(shards):
            block = sums_buf[k, at, :]
            out_ref[k, at, :] = block + below
            step = jnp.where(last, block, 0.0)
            for shift in (32, 16, 8):
                step += pltpu.roll(step, LANES - shift, 1)
            below += step
        return 0

    def both_stages(g, _):
        for j in range(8 // GROUP):
            some_features(g * (8 // GROUP) + j, 0)
        return eight_features(jnp.maximum(g - 1, 0), 0)

    lax.fori_loop(0, feats // 8, both_stages, 0, unroll=UNROLL)
    eight_features(feats // 8 - 1, 0)
    final = out_ref[shards - 1, 0:8, :]
    for k in range(shards):
        out_ref[k, feats : feats + 8, :] = final


def gain_kernel(got_ref, out_ref):
    shards, feats = got_ref.shape[0], got_ref.shape[1] - 8
    left = got_ref[0]
    for k in range(1, shards):
        left += got_ref[k]
    total = left[feats : feats + 1, :]
    left = left[:feats]
    last = iota((1, LANES), 1) % (LANES // 2) >= LANES // 2 - NODES
    total = jnp.where(last, total, 0.0)
    for shift in (32, 16, 8):
        total += pltpu.roll(total, LANES - shift, 1)
    grad, hess = left, pltpu.roll(left, LANES // 2, 1)
    grad_all, hess_all = total, pltpu.roll(total, LANES // 2, 1)
    gain = (
        grad * grad / (hess + 1.0)
        + (grad_all - grad) * (grad_all - grad) / (hess_all - hess + 1.0)
        - grad_all * grad_all / (hess_all + 1.0)
    )
    gain = jnp.where(iota(gain.shape, 1) < LANES // 2, gain, 0.0)
    shape = (NODES * 8, LANES)
    spot, lane = iota(shape, 0), iota(shape, 1)
    chosen = as_ones(lane == (spot % 8) * NODES + spot // 8)
    turned = None
    for part in thirds(gain):
        one = lax.dot_general(
            chosen, part, (((1,), (1,)), ((), ())), preferred_element_type=F32
        )
        turned = one if turned is None else turned + one
    for n in range(NODES):
        out_ref[n] = turned[n * 8 : (n + 1) * 8, :]


def call(kernel, outs, n_in, name, scratch=(), space=pltpu.VMEM, limit=48 << 20):
    vmem = pl.BlockSpec(memory_space=pltpu.VMEM)
    return pl.pallas_call(
        kernel,
        out_shape=outs,
        in_specs=[pl.BlockSpec(memory_space=space)] * n_in,
        out_specs=jax.tree.map(lambda _: vmem, outs),
        scratch_shapes=scratch,
        compiler_params=pltpu.CompilerParams(vmem_limit_bytes=limit),
        name=name,
    )


def exchange(blocks, axes):
    return lax.all_to_all(blocks, axes, 0, 0, tiled=True)


def shards(predictor, events, tie_groups, node_ids, bin_index):
    shape = jax.ShapeDtypeStruct
    n_row, n_feat = lax.axis_size(ROW), lax.axis_size(FEAT)
    quarter = predictor.shape[0] // LANES
    rows = quarter * n_feat
    feats, length = bin_index.shape
    lines = [a.reshape(quarter, LANES) for a in (predictor, events, tie_groups)]
    spread = call(
        spread_kernel,
        shape((n_feat, 3 * quarter, LANES), F32),
        3,
        "spread",
        [pltpu.VMEM(a.shape, a.dtype) for a in lines] + [pltpu.SemaphoreType.DMA((3,))],
        pl.ANY,
        67_000_000,
    )(*lines)
    got = exchange(spread, FEAT)
    message, own = call(
        risk_kernel,
        (shape((n_row, rows, LANES), F32), shape((4, rows, LANES), F32)),
        1,
        "risk",
    )(got)
    received = exchange(message, ROW)
    hi = (bin_index // 8).astype(F32)
    lo = (bin_index % 8).astype(F32)
    gradient, hessian, left = call(
        hist_kernel,
        (
            shape((quarter, LANES), F32),
            shape((quarter, LANES), F32),
            shape((n_row, feats + 8, LANES), F32),
        ),
        5,
        "hist",
        (
            pltpu.VMEM((rows, LANES), F32),
            pltpu.VMEM((rows, LANES), F32),
            pltpu.VMEM((2, 2 * NODES, length), BF),
            pltpu.VMEM((2 * NODES, length), BF),
            pltpu.VMEM((n_row, feats, LANES), F32),
        ),
    )(received, own, node_ids.reshape(rows, LANES), hi, lo)
    summed = exchange(left, ROW)
    gain = call(gain_kernel, shape((NODES, 8, feats), F32), 1, "gain")(summed)
    return gradient.reshape(-1), hessian.reshape(-1), gain.transpose(0, 2, 1)


def solution(mesh):
    finer = Mesh(mesh.devices.reshape(4, 8, 4, 2), ROW_FEAT)
    in_specs = (P(ROW_FEAT), P(ROW_FEAT), P(ROW_FEAT), P(ROW), P(FEAT, ROW))
    out_specs = (P(ROW_FEAT), P(ROW_FEAT), P(None, FEAT, ROW))
    return jax.shard_map(
        shards, mesh=finer, in_specs=in_specs, out_specs=out_specs, check_vma=False
    )
```

```python
import jax
import jax.numpy as jnp
from jax import lax
from jax.experimental import pallas as pl
from jax.experimental.pallas import tpu as pltpu
from jax.sharding import Mesh
from jax.sharding import PartitionSpec as P

NODES = 8
LANES = 128
FEAT = ("feat_0", "feat_1")
ROW = ("row_0", "row_1")
ROW_FEAT = ROW + FEAT
BF = jnp.bfloat16
F32 = jnp.float32
CHUNK = 512
GROUP = 2


def iota(shape, dim):
    return lax.broadcasted_iota(jnp.int32, shape, dim)


def thirds(x):
    first = x.astype(BF)
    left = x - first.astype(F32)
    second = left.astype(BF)
    third = (left - second.astype(F32)).astype(BF)
    return first, second, third


def times_right(x, ones):
    rows = x.shape[0]
    y = jnp.dot(jnp.concatenate(thirds(x), 0), ones, preferred_element_type=F32)
    return y[:rows] + y[rows : 2 * rows] + y[2 * rows :]


def times_left(ones, x):
    width = x.shape[1]
    y = jnp.dot(ones, jnp.concatenate(thirds(x), 1), preferred_element_type=F32)
    return y[:, :width] + y[:, width : 2 * width] + y[:, 2 * width :]


def as_ones(mask):
    return jnp.where(mask, 1.0, 0.0).astype(BF)


def spread_kernel(pred_ref, ev_ref, tie_ref, out_ref, pred, ev, tie, sems):
    copies = [
        pltpu.make_async_copy(source, target, sems.at[k])
        for k, (source, target) in enumerate(
            ((pred_ref, pred), (ev_ref, ev), (tie_ref, tie))
        )
    ]
    for copy in copies:
        copy.start()
    for copy in copies:
        copy.wait()
    three = jnp.concatenate(
        [pred[...], ev[...].astype(F32), tie[...].astype(F32)], 0
    )
    for k in range(out_ref.shape[0]):
        out_ref[k] = three


def risk_kernel(got_ref, msg_ref, own_ref):
    blocks, quarter = got_ref.shape[0], got_ref.shape[1] // 3
    rows = blocks * quarter
    for k in range(blocks):
        for j in range(3):
            own_ref[j, k * quarter : (k + 1) * quarter, :] = got_ref[
                k, j * quarter : (j + 1) * quarter, :
            ]
    hazard = jnp.exp(own_ref[0])
    tie = own_ref[2]
    own_ref[0] = hazard
    lanes = (LANES, LANES)
    inside = times_right(hazard, as_ones(iota(lanes, 0) >= iota(lanes, 1)))
    totals = jnp.broadcast_to(inside[:, 0:1], inside.shape)
    square = (rows, rows)
    suffix = inside + times_left(as_ones(iota(square, 1) > iota(square, 0)), totals)
    place = iota((rows, LANES), 1) % 8
    first = suffix
    for k in (1, 2, 4):
        same = (pltpu.roll(tie, k, 1) == tie) & (place >= k)
        first = jnp.where(same, pltpu.roll(first, k, 1), first)
    own_ref[3] = first
    signed = jnp.where(own_ref[1] > 0.5, first, -first)
    for k in range(msg_ref.shape[0]):
        msg_ref[k] = signed


def hist_kernel(
    got_ref, own_ref, node_ref, hi_ref, lo_ref,
    grad_ref, hess_ref, out_ref, grad_buf, hess_buf, stat_buf, node_buf, sums_buf,
):
    shards, rows = got_ref.shape[0], own_ref.shape[1]
    row, feat = lax.axis_index(ROW), lax.axis_index(FEAT)
    later = own_later = jnp.zeros((1, LANES), F32)
    sum_one = sum_two = jnp.zeros((rows, LANES), F32)
    for k in reversed(range(shards)):
        value = got_ref[k]
        total = jnp.broadcast_to(jnp.abs(value[0:1, 0:1]), (1, LANES))
        weight = jnp.where((value > 0.0) & (k < row), 1.0 / (value + later), 0.0)
        sum_one += weight
        sum_two += weight * weight
        own_later = jnp.where(k > row, own_later + total, own_later)
        later += total

    def whole(x):
        return jnp.sum(jnp.sum(x, 0, keepdims=True), 1, keepdims=True)

    hazard, failed, tie = own_ref[0], own_ref[1], own_ref[2]
    risk = own_ref[3] + own_later
    one = failed / risk
    both = jnp.concatenate([one, failed / (risk * risk)], 0)
    lanes = (LANES, LANES)
    inside = times_right(both, as_ones(iota(lanes, 0) <= iota(lanes, 1)))
    totals = jnp.broadcast_to(inside[:, LANES - 1 : LANES], inside.shape)
    square = (2 * rows, 2 * rows)
    earlier = (iota(square, 1) < iota(square, 0)) & (
        iota(square, 1) // rows == iota(square, 0) // rows
    )
    upto = inside + times_left(as_ones(earlier), totals)
    haz_one = upto[:rows] + whole(sum_one)
    haz_two = upto[rows:] + whole(sum_two)
    place = iota((rows, LANES), 1) % 8
    for k in (1, 2, 4):
        same = (pltpu.roll(tie, LANES - k, 1) == tie) & (place < 8 - k)
        haz_one = jnp.where(same, pltpu.roll(haz_one, LANES - k, 1), haz_one)
        haz_two = jnp.where(same, pltpu.roll(haz_two, LANES - k, 1), haz_two)
    gradient = hazard * haz_one - failed
    hessian = hazard * haz_one - hazard * hazard * haz_two
    grad_buf[...] = gradient
    hess_buf[...] = hessian
    quarter = grad_ref.shape[0]
    grad_ref[...] = grad_buf[pl.ds(feat * quarter, quarter), :]
    hess_ref[...] = hess_buf[pl.ds(feat * quarter, quarter), :]

    wide = (2 * NODES, LANES)
    levels = iota(wide, 0) % NODES
    for k in range(rows):
        cols = slice(k * LANES, (k + 1) * LANES)
        node_buf[:, cols] = as_ones(node_ref[k : k + 1, :] == levels)
        for j, stat in enumerate((gradient, hessian)):
            stat_buf[j, :, cols] = jnp.broadcast_to(stat[k : k + 1, :], wide).astype(BF)

    feats, length = hi_ref.shape
    tops = iota((shards, CHUNK), 0).astype(F32).astype(BF)
    bins = (iota((8 * NODES, CHUNK), 0) // NODES).astype(F32).astype(BF)
    zero = jnp.zeros((), BF)
    half = iota((shards, LANES), 1) < LANES // 2

    def some_features(g):
        acc = None
        for c in range(length // CHUNK):
            cols = pl.ds(c * CHUNK, CHUNK)
            node = jnp.concatenate([node_buf[:, cols]] * 4, 0)
            grad = jnp.concatenate([stat_buf[0, :, cols]] * 2, 0)
            hess = jnp.concatenate([stat_buf[1, :, cols]] * 2, 0)
            upper, lower = [], []
            for j in range(GROUP):
                at = pl.ds(g * GROUP + j, 1)
                lo = jnp.broadcast_to(lo_ref[at, cols], (2 * NODES, CHUNK)).astype(BF)
                hi = jnp.broadcast_to(hi_ref[at, cols], (2 * NODES, CHUNK)).astype(BF)
                top = jnp.concatenate([hi] * 2, 0) == tops
                upper += [jnp.where(top, grad, zero), jnp.where(top, hess, zero)]
                reached = jnp.concatenate([lo] * 4, 0) <= bins
                lower.append(jnp.where(reached, node, zero))
            part = lax.dot_general(
                jnp.concatenate(upper, 0), jnp.concatenate(lower, 0),
                (((1,), (1,)), ((), ())), preferred_element_type=F32,
            )
            acc = part if acc is None else acc + part
        for j in range(GROUP):
            rows_of = slice(2 * shards * j, 2 * shards * (j + 1))
            lanes_of = slice(LANES * (j // 2), LANES * (j // 2 + 1))
            both = acc[rows_of, lanes_of]
            grad, hess = both[:shards], both[shards:]
            if j % 2 == 0:
                hess = pltpu.roll(hess, LANES // 2, 1)
            else:
                grad = pltpu.roll(grad, LANES // 2, 1)
            sums_buf[:, g * GROUP + j, :] = jnp.where(half, grad, hess)

    last = iota((8, LANES), 1) % (LANES // 2) >= LANES // 2 - NODES

    def eight_features(g):
        at = pl.ds(g * 8, 8)
        below = jnp.zeros((8, LANES), F32)
        for k in range(shards):
            block = sums_buf[k, at, :]
            out_ref[k, at, :] = block + below
            step = jnp.where(last, block, 0.0)
            for shift in (32, 16, 8):
                step += pltpu.roll(step, LANES - shift, 1)
            below += step

    for g in range(feats // 8):
        for j in range(8 // GROUP):
            some_features(g * (8 // GROUP) + j)
        if g:
            eight_features(g - 1)
    eight_features(feats // 8 - 1)
    final = out_ref[shards - 1, 0:8, :]
    for k in range(shards):
        out_ref[k, feats : feats + 8, :] = final


def gain_kernel(got_ref, out_ref):
    shards, feats = got_ref.shape[0], got_ref.shape[1] - 8
    left = got_ref[0]
    for k in range(1, shards):
        left += got_ref[k]
    total = left[feats : feats + 1, :]
    left = left[:feats]
    last = iota((1, LANES), 1) % (LANES // 2) >= LANES // 2 - NODES
    total = jnp.where(last, total, 0.0)
    for shift in (32, 16, 8):
        total += pltpu.roll(total, LANES - shift, 1)
    grad, hess = left, pltpu.roll(left, LANES // 2, 1)
    grad_all, hess_all = total, pltpu.roll(total, LANES // 2, 1)
    gain = (
        grad * grad / (hess + 1.0)
        + (grad_all - grad) * (grad_all - grad) / (hess_all - hess + 1.0)
        - grad_all * grad_all / (hess_all + 1.0)
    )
    gain = jnp.where(iota(gain.shape, 1) < LANES // 2, gain, 0.0)
    shape = (NODES * 8, LANES)
    spot, lane = iota(shape, 0), iota(shape, 1)
    chosen = as_ones(lane == (spot % 8) * NODES + spot // 8)
    turned = None
    for part in thirds(gain):
        one = lax.dot_general(
            chosen, part, (((1,), (1,)), ((), ())), preferred_element_type=F32
        )
        turned = one if turned is None else turned + one
    for n in range(NODES):
        out_ref[n] = turned[n * 8 : (n + 1) * 8, :]


def call(kernel, outs, n_in, name, scratch=(), space=pltpu.VMEM, limit=48 << 20):
    vmem = pl.BlockSpec(memory_space=pltpu.VMEM)
    return pl.pallas_call(
        kernel,
        out_shape=outs,
        in_specs=[pl.BlockSpec(memory_space=space)] * n_in,
        out_specs=jax.tree.map(lambda _: vmem, outs),
        scratch_shapes=scratch,
        compiler_params=pltpu.CompilerParams(vmem_limit_bytes=limit),
        name=name,
    )


def exchange(blocks, axes):
    return lax.all_to_all(blocks, axes, 0, 0, tiled=True)


def shards(predictor, events, tie_groups, node_ids, bin_index):
    shape = jax.ShapeDtypeStruct
    n_row, n_feat = lax.axis_size(ROW), lax.axis_size(FEAT)
    quarter = predictor.shape[0] // LANES
    rows = quarter * n_feat
    feats, length = bin_index.shape
    lines = [a.reshape(quarter, LANES) for a in (predictor, events, tie_groups)]
    spread = call(
        spread_kernel,
        shape((n_feat, 3 * quarter, LANES), F32),
        3,
        "spread",
        [pltpu.VMEM(a.shape, a.dtype) for a in lines] + [pltpu.SemaphoreType.DMA((3,))],
        pl.ANY,
        67_000_000,
    )(*lines)
    got = exchange(spread, FEAT)
    message, own = call(
        risk_kernel,
        (shape((n_row, rows, LANES), F32), shape((4, rows, LANES), F32)),
        1,
        "risk",
    )(got)
    received = exchange(message, ROW)
    hi = (bin_index // 8).astype(F32)
    lo = (bin_index % 8).astype(F32)
    gradient, hessian, left = call(
        hist_kernel,
        (
            shape((quarter, LANES), F32),
            shape((quarter, LANES), F32),
            shape((n_row, feats + 8, LANES), F32),
        ),
        5,
        "hist",
        (
            pltpu.VMEM((rows, LANES), F32),
            pltpu.VMEM((rows, LANES), F32),
            pltpu.VMEM((2, 2 * NODES, length), BF),
            pltpu.VMEM((2 * NODES, length), BF),
            pltpu.VMEM((n_row, feats, LANES), F32),
        ),
    )(received, own, node_ids.reshape(rows, LANES), hi, lo)
    summed = exchange(left, ROW)
    gain = call(gain_kernel, shape((NODES, 8, feats), F32), 1, "gain")(summed)
    return gradient.reshape(-1), hessian.reshape(-1), gain.transpose(0, 2, 1)


def solution(mesh):
    finer = Mesh(mesh.devices.reshape(4, 8, 4, 2), ROW_FEAT)
    in_specs = (P(ROW_FEAT), P(ROW_FEAT), P(ROW_FEAT), P(ROW), P(FEAT, ROW))
    out_specs = (P(ROW_FEAT), P(ROW_FEAT), P(None, FEAT, ROW))
    return jax.shard_map(
        shards, mesh=finer, in_specs=in_specs, out_specs=out_specs, check_vma=False
    )
```

```python
import jax
import jax.numpy as jnp
from jax import lax
from jax.experimental import pallas as pl
from jax.experimental.pallas import tpu as pltpu
from jax.sharding import Mesh
from jax.sharding import PartitionSpec as P

NODES = 8
LANES = 128
FEAT = ("feat_0", "feat_1")
ROW = ("row_0", "row_1")
ROW_FEAT = ROW + FEAT
BF = jnp.bfloat16
F32 = jnp.float32
CHUNK = 512
GROUP = 2


def iota(shape, dim):
    return lax.broadcasted_iota(jnp.int32, shape, dim)


def thirds(x):
    first = x.astype(BF)
    left = x - first.astype(F32)
    second = left.astype(BF)
    third = (left - second.astype(F32)).astype(BF)
    return first, second, third


def times_right(x, ones):
    rows = x.shape[0]
    y = jnp.dot(jnp.concatenate(thirds(x), 0), ones, preferred_element_type=F32)
    return y[:rows] + y[rows : 2 * rows] + y[2 * rows :]


def times_left(ones, x):
    width = x.shape[1]
    y = jnp.dot(ones, jnp.concatenate(thirds(x), 1), preferred_element_type=F32)
    return y[:, :width] + y[:, width : 2 * width] + y[:, 2 * width :]


def as_ones(mask):
    return jnp.where(mask, 1.0, 0.0).astype(BF)


def spread_kernel(pred_ref, ev_ref, tie_ref, out_ref, pred, ev, tie, sems):
    copies = [
        pltpu.make_async_copy(source, target, sems.at[k])
        for k, (source, target) in enumerate(
            ((pred_ref, pred), (ev_ref, ev), (tie_ref, tie))
        )
    ]
    for copy in copies:
        copy.start()
    for copy in copies:
        copy.wait()
    three = jnp.concatenate(
        [pred[...], ev[...].astype(F32), tie[...].astype(F32)], 0
    )
    for k in range(out_ref.shape[0]):
        out_ref[k] = three


def risk_kernel(got_ref, msg_ref, own_ref):
    blocks, quarter = got_ref.shape[0], got_ref.shape[1] // 3
    rows = blocks * quarter
    for k in range(blocks):
        for j in range(3):
            own_ref[j, k * quarter : (k + 1) * quarter, :] = got_ref[
                k, j * quarter : (j + 1) * quarter, :
            ]
    hazard = jnp.exp(own_ref[0])
    tie = own_ref[2]
    own_ref[0] = hazard
    lanes = (LANES, LANES)
    inside = times_right(hazard, as_ones(iota(lanes, 0) >= iota(lanes, 1)))
    totals = jnp.broadcast_to(inside[:, 0:1], inside.shape)
    square = (rows, rows)
    suffix = inside + times_left(as_ones(iota(square, 1) > iota(square, 0)), totals)
    place = iota((rows, LANES), 1) % 8
    first = suffix
    for k in (1, 2, 4):
        same = (pltpu.roll(tie, k, 1) == tie) & (place >= k)
        first = jnp.where(same, pltpu.roll(first, k, 1), first)
    own_ref[3] = first
    signed = jnp.where(own_ref[1] > 0.5, first, -first)
    for k in range(msg_ref.shape[0]):
        msg_ref[k] = signed


def hist_kernel(
    got_ref, own_ref, node_ref, hi_ref, lo_ref,
    grad_ref, hess_ref, out_ref, grad_buf, hess_buf, stat_buf, node_buf, sums_buf,
):
    shards, rows = got_ref.shape[0], own_ref.shape[1]
    row, feat = lax.axis_index(ROW), lax.axis_index(FEAT)
    later = own_later = jnp.zeros((1, LANES), F32)
    sum_one = sum_two = jnp.zeros((rows, LANES), F32)
    for k in reversed(range(shards)):
        value = got_ref[k]
        total = jnp.broadcast_to(jnp.abs(value[0:1, 0:1]), (1, LANES))
        weight = jnp.where((value > 0.0) & (k < row), 1.0 / (value + later), 0.0)
        sum_one += weight
        sum_two += weight * weight
        own_later = jnp.where(k > row, own_later + total, own_later)
        later += total

    def whole(x):
        return jnp.sum(jnp.sum(x, 0, keepdims=True), 1, keepdims=True)

    hazard, failed, tie = own_ref[0], own_ref[1], own_ref[2]
    risk = own_ref[3] + own_later
    one = failed / risk
    both = jnp.concatenate([one, failed / (risk * risk)], 0)
    lanes = (LANES, LANES)
    inside = times_right(both, as_ones(iota(lanes, 0) <= iota(lanes, 1)))
    totals = jnp.broadcast_to(inside[:, LANES - 1 : LANES], inside.shape)
    square = (2 * rows, 2 * rows)
    earlier = (iota(square, 1) < iota(square, 0)) & (
        iota(square, 1) // rows == iota(square, 0) // rows
    )
    upto = inside + times_left(as_ones(earlier), totals)
    haz_one = upto[:rows] + whole(sum_one)
    haz_two = upto[rows:] + whole(sum_two)
    place = iota((rows, LANES), 1) % 8
    for k in (1, 2, 4):
        same = (pltpu.roll(tie, LANES - k, 1) == tie) & (place < 8 - k)
        haz_one = jnp.where(same, pltpu.roll(haz_one, LANES - k, 1), haz_one)
        haz_two = jnp.where(same, pltpu.roll(haz_two, LANES - k, 1), haz_two)
    gradient = hazard * haz_one - failed
    hessian = hazard * haz_one - hazard * hazard * haz_two
    grad_buf[...] = gradient
    hess_buf[...] = hessian
    quarter = grad_ref.shape[0]
    grad_ref[...] = grad_buf[pl.ds(feat * quarter, quarter), :]
    hess_ref[...] = hess_buf[pl.ds(feat * quarter, quarter), :]

    wide = (2 * NODES, LANES)
    levels = iota(wide, 0) % NODES
    for k in range(rows):
        cols = slice(k * LANES, (k + 1) * LANES)
        node_buf[:, cols] = as_ones(node_ref[k : k + 1, :] == levels)
        for j, stat in enumerate((gradient, hessian)):
            stat_buf[j, :, cols] = jnp.broadcast_to(stat[k : k + 1, :], wide).astype(BF)

    feats, length = hi_ref.shape
    tops = iota((shards, CHUNK), 0).astype(F32).astype(BF)
    bins = (iota((8 * NODES, CHUNK), 0) // NODES).astype(F32).astype(BF)
    zero = jnp.zeros((), BF)
    half = iota((shards, LANES), 1) < LANES // 2

    def some_features(g):
        acc = None
        for c in range(length // CHUNK):
            cols = pl.ds(c * CHUNK, CHUNK)
            node = jnp.concatenate([node_buf[:, cols]] * 4, 0)
            grad = jnp.concatenate([stat_buf[0, :, cols]] * 2, 0)
            hess = jnp.concatenate([stat_buf[1, :, cols]] * 2, 0)
            upper, lower = [], []
            for j in range(GROUP):
                at = pl.ds(g * GROUP + j, 1)
                lo = jnp.broadcast_to(lo_ref[at, cols], (2 * NODES, CHUNK)).astype(BF)
                hi = jnp.broadcast_to(hi_ref[at, cols], (2 * NODES, CHUNK)).astype(BF)
                top = jnp.concatenate([hi] * 2, 0) == tops
                upper += [jnp.where(top, grad, zero), jnp.where(top, hess, zero)]
                reached = jnp.concatenate([lo] * 4, 0) <= bins
                lower.append(jnp.where(reached, node, zero))
            part = lax.dot_general(
                jnp.concatenate(upper, 0), jnp.concatenate(lower, 0),
                (((1,), (1,)), ((), ())), preferred_element_type=F32,
            )
            acc = part if acc is None else acc + part
        for j in range(GROUP):
            rows_of = slice(2 * shards * j, 2 * shards * (j + 1))
            lanes_of = slice(LANES * (j // 2), LANES * (j // 2 + 1))
            both = acc[rows_of, lanes_of]
            grad, hess = both[:shards], both[shards:]
            if j % 2 == 0:
                hess = pltpu.roll(hess, LANES // 2, 1)
            else:
                grad = pltpu.roll(grad, LANES // 2, 1)
            sums_buf[:, g * GROUP + j, :] = jnp.where(half, grad, hess)

    last = iota((8, LANES), 1) % (LANES // 2) >= LANES // 2 - NODES

    def eight_features(g):
        at = pl.ds(g * 8, 8)
        below = jnp.zeros((8, LANES), F32)
        for k in range(shards):
            block = sums_buf[k, at, :]
            done = block + below
            out_ref[k, 2 * g] = done[:4]
            out_ref[k, 2 * g + 1] = done[4:]
            step = jnp.where(last, block, 0.0)
            for shift in (32, 16, 8):
                step += pltpu.roll(step, LANES - shift, 1)
            below += step

    for g in range(feats // 8):
        for j in range(8 // GROUP):
            some_features(g * (8 // GROUP) + j)
        if g:
            eight_features(g - 1)
    eight_features(feats // 8 - 1)
    final = out_ref[shards - 1, 0]
    for k in range(shards):
        out_ref[k, feats // 4] = final


def gain_kernel(got_ref, out_ref):
    shards, quads = got_ref.shape[0], got_ref.shape[1]
    pieces = []
    for q in range(quads):
        piece = got_ref[0, q]
        for k in range(1, shards):
            piece += got_ref[k, q]
        pieces.append(piece)
    total = pieces[-1][0:1, :]
    left = jnp.concatenate(pieces[:-1], 0)
    last = iota((1, LANES), 1) % (LANES // 2) >= LANES // 2 - NODES
    total = jnp.where(last, total, 0.0)
    for shift in (32, 16, 8):
        total += pltpu.roll(total, LANES - shift, 1)
    grad, hess = left, pltpu.roll(left, LANES // 2, 1)
    grad_all, hess_all = total, pltpu.roll(total, LANES // 2, 1)
    gain = (
        grad * grad / (hess + 1.0)
        + (grad_all - grad) * (grad_all - grad) / (hess_all - hess + 1.0)
        - grad_all * grad_all / (hess_all + 1.0)
    )
    gain = jnp.where(iota(gain.shape, 1) < LANES // 2, gain, 0.0)
    shape = (NODES * 8, LANES)
    spot, lane = iota(shape, 0), iota(shape, 1)
    chosen = as_ones(lane == (spot % 8) * NODES + spot // 8)
    turned = None
    for part in thirds(gain):
        one = lax.dot_general(
            chosen, part, (((1,), (1,)), ((), ())), preferred_element_type=F32
        )
        turned = one if turned is None else turned + one
    for n in range(NODES):
        out_ref[n] = turned[n * 8 : (n + 1) * 8, :]


def call(kernel, outs, n_in, name, scratch=(), space=pltpu.VMEM, limit=48 << 20):
    vmem = pl.BlockSpec(memory_space=pltpu.VMEM)
    return pl.pallas_call(
        kernel,
        out_shape=outs,
        in_specs=[pl.BlockSpec(memory_space=space)] * n_in,
        out_specs=jax.tree.map(lambda _: vmem, outs),
        scratch_shapes=scratch,
        compiler_params=pltpu.CompilerParams(vmem_limit_bytes=limit),
        name=name,
    )


def exchange(blocks, axes):
    return lax.all_to_all(blocks, axes, 0, 0, tiled=True)


def shards(predictor, events, tie_groups, node_ids, bin_index):
    shape = jax.ShapeDtypeStruct
    n_row, n_feat = lax.axis_size(ROW), lax.axis_size(FEAT)
    quarter = predictor.shape[0] // LANES
    rows = quarter * n_feat
    feats, length = bin_index.shape
    lines = [a.reshape(quarter, LANES) for a in (predictor, events, tie_groups)]
    spread = call(
        spread_kernel,
        shape((n_feat, 3 * quarter, LANES), F32),
        3,
        "spread",
        [pltpu.VMEM(a.shape, a.dtype) for a in lines] + [pltpu.SemaphoreType.DMA((3,))],
        pl.ANY,
        67_000_000,
    )(*lines)
    got = exchange(spread, FEAT)
    message, own = call(
        risk_kernel,
        (shape((n_row, rows, LANES), F32), shape((4, rows, LANES), F32)),
        1,
        "risk",
    )(got)
    received = exchange(message, ROW)
    hi = (bin_index // 8).astype(F32)
    lo = (bin_index % 8).astype(F32)
    gradient, hessian, left = call(
        hist_kernel,
        (
            shape((quarter, LANES), F32),
            shape((quarter, LANES), F32),
            shape((n_row, feats // 4 + 1, 4, LANES), F32),
        ),
        5,
        "hist",
        (
            pltpu.VMEM((rows, LANES), F32),
            pltpu.VMEM((rows, LANES), F32),
            pltpu.VMEM((2, 2 * NODES, length), BF),
            pltpu.VMEM((2 * NODES, length), BF),
            pltpu.VMEM((n_row, feats, LANES), F32),
        ),
    )(received, own, node_ids.reshape(rows, LANES), hi, lo)
    summed = exchange(left, ROW)
    gain = call(gain_kernel, shape((NODES, 8, feats), F32), 1, "gain")(summed)
    return gradient.reshape(-1), hessian.reshape(-1), gain.transpose(0, 2, 1)


def solution(mesh):
    finer = Mesh(mesh.devices.reshape(4, 8, 4, 2), ROW_FEAT)
    in_specs = (P(ROW_FEAT), P(ROW_FEAT), P(ROW_FEAT), P(ROW), P(FEAT, ROW))
    out_specs = (P(ROW_FEAT), P(ROW_FEAT), P(None, FEAT, ROW))
    return jax.shard_map(
        shards, mesh=finer, in_specs=in_specs, out_specs=out_specs, check_vma=False
    )
```

```python
import jax
import jax.numpy as jnp
from jax import lax
from jax.experimental import pallas as pl
from jax.experimental.pallas import tpu as pltpu
from jax.sharding import Mesh
from jax.sharding import PartitionSpec as P

NODES = 8
LANES = 128
FEAT = ("feat_0", "feat_1")
ROW = ("row_0", "row_1")
ROW_FEAT = ROW + FEAT
BF = jnp.bfloat16
F32 = jnp.float32
CHUNK = 1024
GROUP = 2


def iota(shape, dim):
    return lax.broadcasted_iota(jnp.int32, shape, dim)


def thirds(x):
    first = x.astype(BF)
    left = x - first.astype(F32)
    second = left.astype(BF)
    third = (left - second.astype(F32)).astype(BF)
    return first, second, third


def times_right(x, ones):
    rows = x.shape[0]
    y = jnp.dot(jnp.concatenate(thirds(x), 0), ones, preferred_element_type=F32)
    return y[:rows] + y[rows : 2 * rows] + y[2 * rows :]


def times_left(ones, x):
    width = x.shape[1]
    y = jnp.dot(ones, jnp.concatenate(thirds(x), 1), preferred_element_type=F32)
    return y[:, :width] + y[:, width : 2 * width] + y[:, 2 * width :]


def as_ones(mask):
    return jnp.where(mask, 1.0, 0.0).astype(BF)


def spread_kernel(pred_ref, ev_ref, tie_ref, out_ref, pred, ev, tie, sems):
    copies = [
        pltpu.make_async_copy(source, target, sems.at[k])
        for k, (source, target) in enumerate(
            ((pred_ref, pred), (ev_ref, ev), (tie_ref, tie))
        )
    ]
    for copy in copies:
        copy.start()
    for copy in copies:
        copy.wait()
    three = jnp.concatenate(
        [pred[...], ev[...].astype(F32), tie[...].astype(F32)], 0
    )
    for k in range(out_ref.shape[0]):
        out_ref[k] = three


def risk_kernel(got_ref, msg_ref, own_ref):
    blocks, quarter = got_ref.shape[0], got_ref.shape[1] // 3
    rows = blocks * quarter
    for k in range(blocks):
        for j in range(3):
            own_ref[j, k * quarter : (k + 1) * quarter, :] = got_ref[
                k, j * quarter : (j + 1) * quarter, :
            ]
    hazard = jnp.exp(own_ref[0])
    tie = own_ref[2]
    own_ref[0] = hazard
    lanes = (LANES, LANES)
    inside = times_right(hazard, as_ones(iota(lanes, 0) >= iota(lanes, 1)))
    totals = jnp.broadcast_to(inside[:, 0:1], inside.shape)
    square = (rows, rows)
    suffix = inside + times_left(as_ones(iota(square, 1) > iota(square, 0)), totals)
    place = iota((rows, LANES), 1) % 8
    first = suffix
    for k in (1, 2, 4):
        same = (pltpu.roll(tie, k, 1) == tie) & (place >= k)
        first = jnp.where(same, pltpu.roll(first, k, 1), first)
    own_ref[3] = first
    signed = jnp.where(own_ref[1] > 0.5, first, -first)
    for k in range(msg_ref.shape[0]):
        msg_ref[k] = signed


def hist_kernel(
    got_ref, own_ref, node_ref, hi_ref, lo_ref,
    grad_ref, hess_ref, out_ref, grad_buf, hess_buf, stat_buf, node_buf, sums_buf,
):
    shards, rows = got_ref.shape[0], own_ref.shape[1]
    row, feat = lax.axis_index(ROW), lax.axis_index(FEAT)
    later = own_later = jnp.zeros((1, LANES), F32)
    sum_one = sum_two = jnp.zeros((rows, LANES), F32)
    for k in reversed(range(shards)):
        value = got_ref[k]
        total = jnp.broadcast_to(jnp.abs(value[0:1, 0:1]), (1, LANES))
        weight = jnp.where((value > 0.0) & (k < row), 1.0 / (value + later), 0.0)
        sum_one += weight
        sum_two += weight * weight
        own_later = jnp.where(k > row, own_later + total, own_later)
        later += total

    def whole(x):
        return jnp.sum(jnp.sum(x, 0, keepdims=True), 1, keepdims=True)

    hazard, failed, tie = own_ref[0], own_ref[1], own_ref[2]
    risk = own_ref[3] + own_later
    one = failed / risk
    both = jnp.concatenate([one, failed / (risk * risk)], 0)
    lanes = (LANES, LANES)
    inside = times_right(both, as_ones(iota(lanes, 0) <= iota(lanes, 1)))
    totals = jnp.broadcast_to(inside[:, LANES - 1 : LANES], inside.shape)
    square = (2 * rows, 2 * rows)
    earlier = (iota(square, 1) < iota(square, 0)) & (
        iota(square, 1) // rows == iota(square, 0) // rows
    )
    upto = inside + times_left(as_ones(earlier), totals)
    haz_one = upto[:rows] + whole(sum_one)
    haz_two = upto[rows:] + whole(sum_two)
    place = iota((rows, LANES), 1) % 8
    for k in (1, 2, 4):
        same = (pltpu.roll(tie, LANES - k, 1) == tie) & (place < 8 - k)
        haz_one = jnp.where(same, pltpu.roll(haz_one, LANES - k, 1), haz_one)
        haz_two = jnp.where(same, pltpu.roll(haz_two, LANES - k, 1), haz_two)
    gradient = hazard * haz_one - failed
    hessian = hazard * haz_one - hazard * hazard * haz_two
    grad_buf[...] = gradient
    hess_buf[...] = hessian
    quarter = grad_ref.shape[0]
    grad_ref[...] = grad_buf[pl.ds(feat * quarter, quarter), :]
    hess_ref[...] = hess_buf[pl.ds(feat * quarter, quarter), :]

    wide = (2 * NODES, LANES)
    levels = iota(wide, 0) % NODES
    for k in range(rows):
        cols = slice(k * LANES, (k + 1) * LANES)
        node_buf[:, cols] = as_ones(node_ref[k : k + 1, :] == levels)
        for j, stat in enumerate((gradient, hessian)):
            stat_buf[j, :, cols] = jnp.broadcast_to(stat[k : k + 1, :], wide).astype(BF)

    feats, length = hi_ref.shape
    tops = iota((shards, CHUNK), 0).astype(F32).astype(BF)
    bins = (iota((8 * NODES, CHUNK), 0) // NODES).astype(F32).astype(BF)
    zero = jnp.zeros((), BF)
    half = iota((shards, LANES), 1) < LANES // 2

    def some_features(g):
        acc = None
        for c in range(length // CHUNK):
            cols = pl.ds(c * CHUNK, CHUNK)
            node = jnp.concatenate([node_buf[:, cols]] * 4, 0)
            grad = jnp.concatenate([stat_buf[0, :, cols]] * 2, 0)
            hess = jnp.concatenate([stat_buf[1, :, cols]] * 2, 0)
            upper, lower = [], []
            for j in range(GROUP):
                at = pl.ds(g * GROUP + j, 1)
                lo = jnp.broadcast_to(lo_ref[at, cols], (2 * NODES, CHUNK)).astype(BF)
                hi = jnp.broadcast_to(hi_ref[at, cols], (2 * NODES, CHUNK)).astype(BF)
                top = jnp.concatenate([hi] * 2, 0) == tops
                upper += [jnp.where(top, grad, zero), jnp.where(top, hess, zero)]
                reached = jnp.concatenate([lo] * 4, 0) <= bins
                lower.append(jnp.where(reached, node, zero))
            part = lax.dot_general(
                jnp.concatenate(upper, 0), jnp.concatenate(lower, 0),
                (((1,), (1,)), ((), ())), preferred_element_type=F32,
            )
            acc = part if acc is None else acc + part
        for j in range(GROUP):
            rows_of = slice(2 * shards * j, 2 * shards * (j + 1))
            lanes_of = slice(LANES * (j // 2), LANES * (j // 2 + 1))
            both = acc[rows_of, lanes_of]
            grad, hess = both[:shards], both[shards:]
            if j % 2 == 0:
                hess = pltpu.roll(hess, LANES // 2, 1)
            else:
                grad = pltpu.roll(grad, LANES // 2, 1)
            sums_buf[:, g * GROUP + j, :] = jnp.where(half, grad, hess)

    last = iota((8, LANES), 1) % (LANES // 2) >= LANES // 2 - NODES

    def eight_features(g):
        at = pl.ds(g * 8, 8)
        below = jnp.zeros((8, LANES), F32)
        for k in range(shards):
            block = sums_buf[k, at, :]
            done = block + below
            out_ref[k, 2 * g] = done[:4]
            out_ref[k, 2 * g + 1] = done[4:]
            step = jnp.where(last, block, 0.0)
            for shift in (32, 16, 8):
                step += pltpu.roll(step, LANES - shift, 1)
            below += step

    for g in range(feats // 8):
        for j in range(8 // GROUP):
            some_features(g * (8 // GROUP) + j)
        if g:
            eight_features(g - 1)
    eight_features(feats // 8 - 1)
    final = out_ref[shards - 1, 0]
    for k in range(shards):
        out_ref[k, feats // 4] = final


def gain_kernel(got_ref, out_ref):
    shards, quads = got_ref.shape[0], got_ref.shape[1]
    pieces = []
    for q in range(quads):
        piece = got_ref[0, q]
        for k in range(1, shards):
            piece += got_ref[k, q]
        pieces.append(piece)
    total = pieces[-1][0:1, :]
    left = jnp.concatenate(pieces[:-1], 0)
    last = iota((1, LANES), 1) % (LANES // 2) >= LANES // 2 - NODES
    total = jnp.where(last, total, 0.0)
    for shift in (32, 16, 8):
        total += pltpu.roll(total, LANES - shift, 1)
    grad, hess = left, pltpu.roll(left, LANES // 2, 1)
    grad_all, hess_all = total, pltpu.roll(total, LANES // 2, 1)
    gain = (
        grad * grad / (hess + 1.0)
        + (grad_all - grad) * (grad_all - grad) / (hess_all - hess + 1.0)
        - grad_all * grad_all / (hess_all + 1.0)
    )
    gain = jnp.where(iota(gain.shape, 1) < LANES // 2, gain, 0.0)
    shape = (NODES * 8, LANES)
    spot, lane = iota(shape, 0), iota(shape, 1)
    chosen = as_ones(lane == (spot % 8) * NODES + spot // 8)
    turned = None
    for part in thirds(gain):
        one = lax.dot_general(
            chosen, part, (((1,), (1,)), ((), ())), preferred_element_type=F32
        )
        turned = one if turned is None else turned + one
    for n in range(NODES):
        out_ref[n] = turned[n * 8 : (n + 1) * 8, :]


def call(kernel, outs, n_in, name, scratch=(), space=pltpu.VMEM, limit=48 << 20):
    vmem = pl.BlockSpec(memory_space=pltpu.VMEM)
    return pl.pallas_call(
        kernel,
        out_shape=outs,
        in_specs=[pl.BlockSpec(memory_space=space)] * n_in,
        out_specs=jax.tree.map(lambda _: vmem, outs),
        scratch_shapes=scratch,
        compiler_params=pltpu.CompilerParams(vmem_limit_bytes=limit),
        name=name,
    )


def exchange(blocks, axes):
    return lax.all_to_all(blocks, axes, 0, 0, tiled=True)


def shards(predictor, events, tie_groups, node_ids, bin_index):
    shape = jax.ShapeDtypeStruct
    n_row, n_feat = lax.axis_size(ROW), lax.axis_size(FEAT)
    quarter = predictor.shape[0] // LANES
    rows = quarter * n_feat
    feats, length = bin_index.shape
    lines = [a.reshape(quarter, LANES) for a in (predictor, events, tie_groups)]
    spread = call(
        spread_kernel,
        shape((n_feat, 3 * quarter, LANES), F32),
        3,
        "spread",
        [pltpu.VMEM(a.shape, a.dtype) for a in lines] + [pltpu.SemaphoreType.DMA((3,))],
        pl.ANY,
        67_000_000,
    )(*lines)
    got = exchange(spread, FEAT)
    message, own = call(
        risk_kernel,
        (shape((n_row, rows, LANES), F32), shape((4, rows, LANES), F32)),
        1,
        "risk",
    )(got)
    received = exchange(message, ROW)
    hi = (bin_index // 8).astype(F32)
    lo = (bin_index % 8).astype(F32)
    gradient, hessian, left = call(
        hist_kernel,
        (
            shape((quarter, LANES), F32),
            shape((quarter, LANES), F32),
            shape((n_row, feats // 4 + 1, 4, LANES), F32),
        ),
        5,
        "hist",
        (
            pltpu.VMEM((rows, LANES), F32),
            pltpu.VMEM((rows, LANES), F32),
            pltpu.VMEM((2, 2 * NODES, length), BF),
            pltpu.VMEM((2 * NODES, length), BF),
            pltpu.VMEM((n_row, feats, LANES), F32),
        ),
    )(received, own, node_ids.reshape(rows, LANES), hi, lo)
    summed = exchange(left, ROW)
    gain = call(gain_kernel, shape((NODES, 8, feats), F32), 1, "gain")(summed)
    return gradient.reshape(-1), hessian.reshape(-1), gain.transpose(0, 2, 1)


def solution(mesh):
    finer = Mesh(mesh.devices.reshape(4, 8, 4, 2), ROW_FEAT)
    in_specs = (P(ROW_FEAT), P(ROW_FEAT), P(ROW_FEAT), P(ROW), P(FEAT, ROW))
    out_specs = (P(ROW_FEAT), P(ROW_FEAT), P(None, FEAT, ROW))
    return jax.shard_map(
        shards, mesh=finer, in_specs=in_specs, out_specs=out_specs, check_vma=False
    )
```
